32 devices in a mesh: seq: 4 (over x, core), span: 8 (over z, y).
Axes of the slice: x: 2, y: 2, z: 4, core: 2. Of those that a mesh axis runs over, the one named last changes fastest.
Arguments:
- llm_input: bfloat16 [512, 5120], P(('seq', 'span')), may hold values from -6 to 6
- hidden_grad: bfloat16 [512, 32768], P(None, ('seq', 'span')), may hold values from -1.5 to 1.5
- gate_act: bfloat16 [512, 32768], P(None, ('seq', 'span')), may hold values from -6 to 6
- up_weight: bfloat16 [5120, 32768], P(None, ('seq', 'span')), may hold values from -0.078125 to 0.078125
- span_counts: int32 [16], replicated, may hold values from 16 to 48, as said below
- row_ticks: int32 [512], replicated, may hold values from 0 to 47, as said below
- encoder_out: bfloat16 [8, 384, 1280], P('span'), may hold values from -6 to 6
- mlp_input: bfloat16 [8, 384, 1280], P('span'), may hold values from -6 to 6
- post_gain: float32 [1280], replicated, may hold values from 0.5 to 1.5
- post_bias: float32 [1280], replicated, may hold values from -3 to 3
- adapter_in: bfloat16 [5120, 5120], P(None, 'seq'), may hold values from -0.078125 to 0.078125
- adapter_out: bfloat16 [5120, 5120], P('seq'), may hold values from -0.078125 to 0.078125
- expand_weight: bfloat16 [1280, 5120], P(None, 'seq'), may hold values from -0.15625 to 0.15625
- expand_bias: float32 [5120], P('seq'), may hold values from -3 to 3
- contract_weight: bfloat16 [5120, 1280], P('seq'), may hold values from -0.078125 to 0.078125
Outputs:
- gate_act_grad: bfloat16 [512, 32768], P(None, ('seq', 'span'))
- up_weight_grad: bfloat16 [5120, 32768], P(None, ('seq', 'span'))
- adapter_in_grad: bfloat16 [5120, 5120], P('span', 'seq')
- adapter_out_grad: bfloat16 [5120, 5120], P(('seq', 'span'))
- expand_weight_grad: bfloat16 [1280, 5120], P('span', 'seq')
- contract_weight_grad: bfloat16 [5120, 1280], P(('seq', 'span'))
- expand_bias_grad: float32 [5120], P('seq')
- post_gain_grad: float32 [1280], replicated
- post_bias_grad: float32 [1280], replicated
- contract_bias_grad: float32 [1280], replicated
- encoder_out_grad: bfloat16 [8, 384, 1280], P('span', 'seq')
- mlp_input_grad: bfloat16 [8, 384, 1280], P('span', 'seq')
The draws below stay inside these ranges and needn't reach their ends.
Inputs may be any that keep to these rules, and one draw needn't show every extreme that they name: span_counts sums to 512; its largest entry is exactly 48. `row_ticks`: the rows of each span are consecutive in the sequence, spans in order of their number, span k holding span_counts[k] rows; inside a span the tick rises by one from row to row.
All inputs are finite; a program needn't handle non-finite values.
Results may differ from the reference program's by a relative error of at most 0.03.
Values may be sent and summed in bfloat16 or wider, within the bound.
A program may use at most 192 MiB of HBM per device.

```python
import math
import jax
import jax.numpy as jnp
from jax import lax

D = 5120
FF = 32768
AH = 5120
EW = 1280
EF = 5120
STACK = 4
CH_DEV = 2
ROWS = 512
NCHUNK = 16
CAP = 48
OWN_FR = 384
AIN = 5120
N_SPAN = 8


def span_layout(key):
    mean_count = ROWS // NCHUNK
    spread = CAP - mean_count
    pair_count = NCHUNK // 2
    key_moves, key_pick, key_order, key_shift = jax.random.split(jax.random.fold_in(key, 11), 4)
    transfer = jax.random.randint(key_moves, (pair_count,), -spread, spread + 1)
    chosen = jax.random.randint(key_pick, (), 0, pair_count)
    transfer = jnp.where(jnp.arange(pair_count) == chosen, spread, transfer)
    counts = jnp.stack([mean_count + transfer, mean_count - transfer], axis=1).reshape(NCHUNK)
    counts = jax.random.permutation(key_order, counts).astype(jnp.int32)
    offsets = jax.random.randint(key_shift, (NCHUNK,), 0, CAP - counts + 1)
    span_ends = jnp.cumsum(counts)
    starts = span_ends - counts
    positions = jnp.arange(ROWS)
    span_index = jnp.sum((positions[:, None] >= span_ends[None, :]).astype(jnp.int32), axis=1)
    tick_values = offsets[span_index] + positions - starts[span_index]
    return (counts.astype(jnp.int32), tick_values.astype(jnp.int32))


def draw_span_counts(key, part):
    return span_layout(key)[0]


def draw_row_ticks(key, part):
    return span_layout(key)[1]


def steps_of(own_key, extent, cuts, least, largest):
    level = 1.0
    for position, blocks in cuts:
        heights = jax.random.uniform(jax.random.fold_in(jax.random.fold_in(own_key, 6), position), (blocks,), jnp.float32, least / len(cuts), largest / len(cuts))
        level = level * jnp.repeat(jnp.exp(heights), extent[position] // blocks).reshape((-1,) + (1,) * (len(extent) - 1 - position))
    return level


def centred(own_key, shape, scale, most, shards=(), kind=jnp.bfloat16):
    result = scale * jax.random.normal(own_key, shape, jnp.float32)
    if shards:
        result = result * steps_of(own_key, shape, shards, -0.22, 0.18)
    return jnp.clip(result, -most, most).astype(kind)


def setup_inputs(seed: int = 0) -> dict:
    keys = jax.random.split(jax.random.key(seed), 16)
    return {
        "llm_input": centred(keys[0], (ROWS, D), 1.0, 6.0, ((0, 32),)),
        "hidden_grad": centred(keys[1], (ROWS, FF), 0.25, 1.5, ((1, 32),)),
        "gate_act": centred(keys[2], (ROWS, FF), 1.0, 6.0, ((1, 32),)),
        "up_weight": centred(keys[3], (D, FF), D ** -0.5, 0.078125, ((1, 32),)),
        "span_counts": draw_span_counts(jax.random.fold_in(keys[15], 71), 0),
        "row_ticks": draw_row_ticks(jax.random.fold_in(keys[15], 71), 0),
        "encoder_out": centred(keys[6], (N_SPAN, OWN_FR, EW), 1.0, 6.0, ((0, 8),)),
        "mlp_input": centred(keys[7], (N_SPAN, OWN_FR, EW), 1.0, 6.0, ((0, 8),)),
        "post_gain": jnp.clip(1.0 + 0.1 * jax.random.normal(keys[8], (EW,), jnp.float32), 0.5, 1.5),
        "post_bias": centred(keys[9], (EW,), 0.5, 3.0, (), jnp.float32),
        "adapter_in": centred(keys[10], (AIN, AH), AIN ** -0.5, 0.078125, ((1, 4),)),
        "adapter_out": centred(keys[11], (AH, D), AH ** -0.5, 0.078125, ((0, 4),)),
        "expand_weight": centred(keys[12], (EW, EF), EW ** -0.5, 0.15625, ((1, 4),)),
        "expand_bias": centred(keys[13], (EF,), 0.5, 3.0, ((0, 4),), jnp.float32),
        "contract_weight": centred(keys[14], (EF, EW), EF ** -0.5, 0.078125, ((0, 4),)),
    }


EPSILON = 1e-05

def gelu_value(values):
    return 0.5 * values * (1.0 + lax.erf(values * (1.0 / math.sqrt(2.0))))

def gelu_slope(values):
    cumulative = 0.5 * (1.0 + lax.erf(values * (1.0 / math.sqrt(2.0))))
    return cumulative + values * jnp.exp(-0.5 * values * values) * (1.0 / math.sqrt(2.0 * math.pi))

def locate_rows(span_counts, row_ticks, capacity):
    span_ends = jnp.cumsum(span_counts).astype(jnp.int32)
    positions = jnp.arange(row_ticks.shape[0], dtype=jnp.int32)
    span_of = lax.optimization_barrier(jnp.sum((positions[:, None] >= span_ends[None, :]).astype(jnp.int32), axis=1))
    return (span_of * capacity + row_ticks).astype(jnp.int32)

def reference(llm_input, hidden_grad, gate_act, up_weight, span_counts, row_ticks, encoder_out, mlp_input, post_gain, post_bias, adapter_in, adapter_out, expand_weight, expand_bias, contract_weight):
    up_rows = jnp.dot(llm_input, up_weight, preferred_element_type=jnp.float32)
    gate_act_grad = (hidden_grad.astype(jnp.float32) * up_rows).astype(jnp.bfloat16)
    up_grad = (hidden_grad.astype(jnp.float32) * gate_act.astype(jnp.float32)).astype(jnp.bfloat16)
    up_weight_grad = jnp.dot(llm_input.T, up_grad, preferred_element_type=jnp.float32).astype(jnp.bfloat16)
    audio_grad = jnp.dot(up_grad, up_weight.T, preferred_element_type=jnp.float32).astype(jnp.bfloat16)
    groups, frames_each, width = encoder_out.shape
    slots_each = frames_each // STACK
    capacity = slots_each // CH_DEV
    slot_of = locate_rows(span_counts, row_ticks, capacity)
    token_grad = jnp.zeros((groups * slots_each, audio_grad.shape[1]), jnp.bfloat16).at[slot_of].set(audio_grad)
    frames = encoder_out.reshape(groups * frames_each, width).astype(jnp.float32)
    centre = frames - lax.optimization_barrier(jnp.mean(frames, axis=1, keepdims=True))
    rstd = lax.rsqrt(lax.optimization_barrier(jnp.mean(centre * centre, axis=1, keepdims=True)) + EPSILON)
    nhat = centre * rstd
    stacked = (nhat * post_gain + post_bias).reshape(groups * slots_each, STACK * width).astype(jnp.bfloat16)
    pre_act = jnp.dot(stacked, adapter_in, preferred_element_type=jnp.float32)
    activity = gelu_value(pre_act).astype(jnp.bfloat16)
    act_grad = jnp.dot(token_grad, adapter_out.T, preferred_element_type=jnp.float32)
    pre_grad = (act_grad * gelu_slope(pre_act)).astype(jnp.bfloat16)
    normed_grad = jnp.dot(pre_grad, adapter_in.T, preferred_element_type=jnp.float32).reshape(groups * frames_each, width)
    post_gain_grad = lax.optimization_barrier(jnp.sum(normed_grad * nhat, axis=0))
    post_bias_grad = lax.optimization_barrier(jnp.sum(normed_grad, axis=0))
    scaled = normed_grad * post_gain
    resid = rstd * (scaled - lax.optimization_barrier(jnp.mean(scaled, axis=1, keepdims=True)) - nhat * lax.optimization_barrier(jnp.mean(scaled * nhat, axis=1, keepdims=True)))
    resid = resid.astype(jnp.bfloat16)
    contract_bias_grad = lax.optimization_barrier(jnp.sum(resid.astype(jnp.float32), axis=0))
    inputs = mlp_input.reshape(groups * frames_each, width)
    hidden_pre = jnp.dot(inputs, expand_weight, preferred_element_type=jnp.float32) + expand_bias
    hidden_act = gelu_value(hidden_pre).astype(jnp.bfloat16)
    hidden_grad_enc = jnp.dot(resid, contract_weight.T, preferred_element_type=jnp.float32)
    hidden_pre_grad = (hidden_grad_enc * gelu_slope(hidden_pre)).astype(jnp.bfloat16)
    expand_bias_grad = lax.optimization_barrier(jnp.sum(hidden_pre_grad.astype(jnp.float32), axis=0))
    mlp_input_grad = jnp.dot(hidden_pre_grad, expand_weight.T, preferred_element_type=jnp.float32).astype(jnp.bfloat16)
    members = (stacked.reshape(groups, slots_each, -1), pre_grad.reshape(groups, slots_each, -1), activity.reshape(groups, slots_each, -1), token_grad.reshape(groups, slots_each, -1), inputs.reshape(groups, frames_each, -1), hidden_pre_grad.reshape(groups, frames_each, -1), hidden_act.reshape(groups, frames_each, -1), resid.reshape(groups, frames_each, -1))

    def by_group(totals, pieces):
        st_rows, pg_rows, ac_rows, tg_rows, in_rows, hp_rows, ha_rows, re_rows = pieces
        terms = (jnp.dot(st_rows.T, pg_rows, preferred_element_type=jnp.float32), jnp.dot(ac_rows.T, tg_rows, preferred_element_type=jnp.float32), jnp.dot(in_rows.T, hp_rows, preferred_element_type=jnp.float32), jnp.dot(ha_rows.T, re_rows, preferred_element_type=jnp.float32))
        updated = tuple((total + lax.optimization_barrier(term.astype(jnp.bfloat16)).astype(jnp.float32) for total, term in zip(totals, terms)))
        return (updated, None)
    start = (jnp.zeros(adapter_in.shape, jnp.float32), jnp.zeros(adapter_out.shape, jnp.float32), jnp.zeros(expand_weight.shape, jnp.float32), jnp.zeros(contract_weight.shape, jnp.float32))
    sums, _ = lax.scan(by_group, start, members)
    adapter_in_grad = sums[0].astype(jnp.bfloat16)
    adapter_out_grad = sums[1].astype(jnp.bfloat16)
    expand_weight_grad = sums[2].astype(jnp.bfloat16)
    contract_weight_grad = sums[3].astype(jnp.bfloat16)
    return (gate_act_grad, up_weight_grad, adapter_in_grad, adapter_out_grad, expand_weight_grad, contract_weight_grad, expand_bias_grad, post_gain_grad, post_bias_grad, contract_bias_grad, resid.reshape(groups, frames_each, width), mlp_input_grad.reshape(groups, frames_each, width))
```

```python
import math

import jax
import jax.numpy as jnp
from jax import lax
from jax.sharding import PartitionSpec as P

STACK = 4
CH_DEV = 2


EPSILON = 1e-05


def gelu_value(values):
    return 0.5 * values * (1.0 + lax.erf(values * (1.0 / math.sqrt(2.0))))


def gelu_slope(values):
    cumulative = 0.5 * (1.0 + lax.erf(values * (1.0 / math.sqrt(2.0))))
    return cumulative + values * jnp.exp(-0.5 * values * values) * (1.0 / math.sqrt(2.0 * math.pi))


def locate_rows(span_counts, row_ticks, capacity):
    span_ends = jnp.cumsum(span_counts)
    positions = jnp.arange(row_ticks.shape[0], dtype=jnp.int32)
    span_of = jnp.sum((positions[:, None] >= span_ends[None, :]).astype(jnp.int32), axis=1)
    return span_of * capacity + row_ticks


def contract_last(left, right):
    return lax.dot_general(
        left, right, (((1,), (1,)), ((), ())), preferred_element_type=jnp.float32
    )


def contract_first(left, right):
    return lax.dot_general(
        left, right, (((0,), (0,)), ((), ())), preferred_element_type=jnp.float32
    )


def bit_count(axis):
    return lax.axis_size(axis).bit_length() - 1


def own_bit(axis, bit):
    return lax.rem(lax.div(lax.axis_index(axis), 1 << bit), 2)


def swap(value, axis, bit):
    size = lax.axis_size(axis)
    return lax.ppermute(value, axis, [(index, index ^ (1 << bit)) for index in range(size)])


def pair_sum(left, right):
    return (left.astype(jnp.float32) + right.astype(jnp.float32)).astype(jnp.bfloat16)


def halve(value, dim, axis, bit):
    mine = own_bit(axis, bit)
    sent = swap(lax.dynamic_index_in_dim(value, 1 - mine, dim), axis, bit)
    return pair_sum(lax.dynamic_index_in_dim(value, mine, dim), sent)


def scatter_rows(value, steps, dims):
    for axis, bit in steps:
        value = halve(value, dims[(axis, bit)], axis, bit)
    return value.reshape(-1, value.shape[-1])


def scatter_paths(value, dims, orders):
    parts = jnp.split(value, len(orders), axis=-1)
    parts = [scatter_rows(part, order, dims) for part, order in zip(parts, orders)]
    return jnp.concatenate(parts, axis=-1)


def sum_all(value, axis):
    held = halve(value.reshape(2, value.shape[0] // 2, -1), 0, axis, 0)
    for bit in range(1, bit_count(axis)):
        held = pair_sum(held, swap(held, axis, bit))
    other = swap(held, axis, 0)
    first = own_bit(axis, 0) == 0
    return jnp.concatenate(
        (jnp.where(first, held, other), jnp.where(first, other, held)), axis=0
    ).reshape(value.shape)


def per_device(
    llm_input,
    hidden_grad,
    gate_act,
    up_weight,
    span_counts,
    row_ticks,
    encoder_out,
    mlp_input,
    post_gain,
    post_bias,
    adapter_in,
    adapter_out,
    expand_weight,
    expand_bias,
    contract_weight,
):
    both = ("seq", "span")
    rows_all = row_ticks.shape[0]
    piece = lax.all_gather(llm_input, both, axis=0, tiled=True)
    up_grad = (hidden_grad.astype(jnp.float32) * gate_act.astype(jnp.float32)).astype(jnp.bfloat16)
    frames_each = encoder_out.shape[1]
    width = encoder_out.shape[2]
    slots_each = frames_each // STACK
    capacity = slots_each // CH_DEV
    owner_count = lax.axis_size("span")
    seq_count = lax.axis_size("seq")
    seq_index = lax.axis_index("seq")
    slot_of = locate_rows(span_counts, row_ticks, capacity)

    seq_bits, span_bits = bit_count("seq"), bit_count("span")
    bits_all = seq_bits + span_bits
    row_dims = {("seq", bit): seq_bits - 1 - bit for bit in range(seq_bits)}
    row_dims.update({("span", bit): bits_all - 1 - bit for bit in range(span_bits)})
    split_rows = up_grad.reshape((2,) * bits_all + (rows_all >> bits_all, -1))
    core_dim = row_dims[("seq", 0)]
    core = own_bit("seq", 0)
    sent_rows = lax.dynamic_index_in_dim(split_rows, 1 - core, core_dim)
    kept_rows = lax.dynamic_index_in_dim(split_rows, core, core_dim)
    half_shape = sent_rows.shape[:-1] + (up_weight.shape[0],)
    sent_part = contract_last(sent_rows.reshape(rows_all // 2, -1), up_weight).astype(jnp.bfloat16)
    came_part = swap(sent_part, "seq", 0)
    kept_part = contract_last(kept_rows.reshape(rows_all // 2, -1), up_weight)
    audio_half = (kept_part + came_part.astype(jnp.float32)).astype(jnp.bfloat16)
    seq_steps = [("seq", bit) for bit in range(1, seq_bits)]
    near_step = [("span", 0)]
    far_steps = [("span", bit) for bit in range(1, span_bits)]
    audio_mine = scatter_paths(
        audio_half.reshape(half_shape),
        row_dims,
        (seq_steps + near_step + far_steps, near_step + seq_steps + far_steps),
    )
    audio_mine, piece = lax.optimization_barrier((audio_mine, piece))
    audio_grad = lax.all_gather(audio_mine, both, axis=0, tiled=True)

    frames = encoder_out[0].astype(jnp.float32)
    centre = frames - jnp.mean(frames, axis=1, keepdims=True)
    rstd = lax.rsqrt(jnp.mean(centre * centre, axis=1, keepdims=True) + EPSILON)
    nhat = centre * rstd
    stacked = (nhat * post_gain + post_bias).reshape(slots_each, STACK * width).astype(jnp.bfloat16)
    stacked_all = lax.all_to_all(stacked, "span", split_axis=1, concat_axis=0, tiled=True)
    pre_act = jnp.dot(stacked, adapter_in, preferred_element_type=jnp.float32)
    activity = gelu_value(pre_act).astype(jnp.bfloat16)
    activity_all = lax.all_to_all(activity, "span", split_axis=1, concat_axis=0, tiled=True)
    activity_rows = jnp.take(activity_all, slot_of, axis=0)
    inputs = mlp_input[0]
    hidden_pre = jnp.dot(inputs, expand_weight, preferred_element_type=jnp.float32) + expand_bias
    hidden_act = gelu_value(hidden_pre).astype(jnp.bfloat16)

    weight_sum = contract_first(piece, up_grad)
    up_rows = jnp.dot(piece, up_weight, preferred_element_type=jnp.float32)
    gate_act_grad = (hidden_grad.astype(jnp.float32) * up_rows).astype(jnp.bfloat16)
    up_weight_grad = weight_sum.astype(jnp.bfloat16)

    audio_grad, gate_act_grad, up_weight_grad = lax.optimization_barrier(
        (audio_grad, gate_act_grad, up_weight_grad)
    )
    first_slot = lax.axis_index("span") * slots_each
    my_slots = first_slot + jnp.arange(slots_each, dtype=jnp.int32)
    matches = my_slots[:, None] == slot_of[None, :]
    filled = jnp.any(matches, axis=1)
    source = jnp.sum(jnp.where(matches, jnp.arange(rows_all, dtype=jnp.int32)[None, :], 0), axis=1)
    token_grad = jnp.take(audio_grad, source, axis=0) * filled[:, None].astype(jnp.bfloat16)
    act_grad = contract_last(token_grad, adapter_out)
    pre_grad = (act_grad * gelu_slope(pre_act)).astype(jnp.bfloat16)
    stacked_part = contract_last(pre_grad, adapter_in)
    mine_frames = frames_each // seq_count
    normed_grad = (
        sum_all(stacked_part.astype(jnp.bfloat16), "seq")
        .astype(jnp.float32)
        .reshape(frames_each, width)
    )
    pre_all = lax.all_gather(pre_grad, "span", axis=0, tiled=True)
    adapter_out_sum = contract_first(activity_rows, audio_grad)
    adapter_in_sum = contract_first(stacked_all, pre_all)
    scaled = normed_grad * post_gain
    resid = rstd * (
        scaled
        - jnp.mean(scaled, axis=1, keepdims=True)
        - nhat * jnp.mean(scaled * nhat, axis=1, keepdims=True)
    )
    resid = resid.astype(jnp.bfloat16)
    gain_part = jnp.sum(normed_grad * nhat, axis=0)
    shift_part = jnp.sum(normed_grad, axis=0)
    out_bias_part = jnp.sum(resid.astype(jnp.float32), axis=0)
    resid_mine = lax.dynamic_slice_in_dim(resid, seq_index * mine_frames, mine_frames, 0)
    hidden_enc_grad = contract_last(resid, contract_weight)
    hidden_pre_grad = (hidden_enc_grad * gelu_slope(hidden_pre)).astype(jnp.bfloat16)
    in_bias_part = jnp.sum(hidden_pre_grad.astype(jnp.float32), axis=0)
    partial_expand = contract_first(inputs, hidden_pre_grad).astype(jnp.bfloat16)
    partial_contract = contract_first(hidden_act, resid).astype(jnp.bfloat16)
    span_dims = {("span", bit): span_bits - 1 - bit for bit in range(span_bits)}
    contract_sum = scatter_paths(
        partial_contract.reshape(
            (2,) * span_bits + (partial_contract.shape[0] >> span_bits, -1)
        ),
        span_dims,
        (near_step + far_steps, far_steps + near_step),
    )
    expand_sum = lax.psum_scatter(partial_expand, "span", scatter_dimension=0, tiled=True)
    hidden_later, contract_sum = lax.optimization_barrier((hidden_pre_grad, contract_sum))
    mlp_part = contract_last(hidden_later, expand_weight).astype(jnp.bfloat16)
    mlp_input_grad = scatter_rows(
        mlp_part.reshape((2,) * seq_bits + (mine_frames, -1)),
        [("seq", bit) for bit in range(seq_bits)],
        {("seq", bit): seq_bits - 1 - bit for bit in range(seq_bits)},
    )
    part_sums = (in_bias_part, gain_part, shift_part, out_bias_part)
    sums = jnp.concatenate(part_sums)
    for bit in range(span_bits):
        sums = sums + swap(sums, "span", bit)
    expand_bias_grad, post_gain_grad, post_bias_grad, contract_bias_grad = jnp.split(
        sums, (in_bias_part.shape[0], in_bias_part.shape[0] + width, in_bias_part.shape[0] + 2 * width)
    )
    return (
        gate_act_grad,
        up_weight_grad,
        adapter_in_sum.astype(jnp.bfloat16),
        adapter_out_sum.astype(jnp.bfloat16),
        expand_sum,
        contract_sum,
        expand_bias_grad,
        post_gain_grad,
        post_bias_grad,
        contract_bias_grad,
        resid_mine.reshape(1, mine_frames, width),
        mlp_input_grad.reshape(1, mine_frames, width),
    )


def solution(mesh):
    return jax.shard_map(
        per_device,
        mesh=mesh,
        in_specs=(
            P(("seq", "span"), None),
            P(None, ("seq", "span")),
            P(None, ("seq", "span")),
            P(None, ("seq", "span")),
            P(),
            P(),
            P("span", None, None),
            P("span", None, None),
            P(),
            P(),
            P(None, "seq"),
            P("seq", None),
            P(None, "seq"),
            P("seq"),
            P("seq", None),
        ),
        out_specs=(
            P(None, ("seq", "span")),
            P(None, ("seq", "span")),
            P("span", "seq"),
            P(("seq", "span"), None),
            P("span", "seq"),
            P(("seq", "span"), None),
            P("seq"),
            P(),
            P(),
            P(),
            P("span", "seq", None),
            P("span", "seq", None),
        ),
        check_vma=False,
    )
```
